32 devices in a mesh: rep: 2 (over y), shard: 16 (over z, x, core).
Axes of the slice: x: 2, y: 2, z: 4, core: 2. Of those that a mesh axis runs over, the one named last changes fastest.
Arguments:
- latents: bfloat16 [32, 128, 1152], P(('rep', 'shard')), may hold values from -5 to 5
- cond: float32 [32, 1152], P(('rep', 'shard')), may hold values from -6 to 6
- timesteps: int32 [32], P(('rep', 'shard')), may hold values from 0 to 999
- cotangent: bfloat16 [32, 128, 1152], P(('rep', 'shard')), may hold values from -6 to 6
- w_qkv: float32 [1152, 3456], P('shard'), may hold values from -0.11785113 to 0.11785113
- w_proj: float32 [1152, 1152], P('shard'), may hold values from -0.75 to 0.75
- w_fc1: float32 [1152, 4608], P('shard'), may hold values from -0.1875 to 0.1875
- w_fc2: float32 [4608, 1152], P('shard'), may hold values from -0.1875 to 0.1875
- w_ada: float32 [1152, 6912], P(None, 'shard'), may hold values from -0.015625 to 0.015625
- biases: float32 [16128], replicated, may hold values from -3 to 3
- m_qkv: float32 [1152, 3456], P('shard', 'rep'), may hold values from -0.00012272017 to 0.00012272017
- m_proj: float32 [1152, 1152], P('shard', 'rep'), may hold values from -0.00012272017 to 0.00012272017
- m_fc1: float32 [1152, 4608], P('shard', 'rep'), may hold values from -0.00012272017 to 0.00012272017
- m_fc2: float32 [4608, 1152], P('shard', 'rep'), may hold values from -0.00012272017 to 0.00012272017
- m_ada: float32 [1152, 6912], P('rep', 'shard'), may hold values from -0.00012272017 to 0.00012272017
- m_bias: float32 [16128], replicated, may hold values from -0.00012272017 to 0.00012272017
- v_qkv: float32 [1152, 3456], P('shard', 'rep'), may hold values from 4.1834e-11 to 1.67336e-10
- v_proj: float32 [1152, 1152], P('shard', 'rep'), may hold values from 4.1834e-11 to 1.67336e-10
- v_fc1: float32 [1152, 4608], P('shard', 'rep'), may hold values from 4.1834e-11 to 1.67336e-10
- v_fc2: float32 [4608, 1152], P('shard', 'rep'), may hold values from 4.1834e-11 to 1.67336e-10
- v_ada: float32 [1152, 6912], P('rep', 'shard'), may hold values from 4.1834e-11 to 1.67336e-10
- v_bias: float32 [16128], replicated, may hold values from 4.1834e-11 to 1.67336e-10
Outputs:
- block_out: float32 [32, 128, 1152], P(('rep', 'shard'))
- latents_grad: float32 [32, 128, 1152], P(('rep', 'shard'))
- cond_grad: float32 [32, 1152], P(('rep', 'shard'))
- new_qkv: float32 [1152, 3456], P('shard')
- new_proj: float32 [1152, 1152], P('shard')
- new_fc1: float32 [1152, 4608], P('shard')
- new_fc2: float32 [4608, 1152], P('shard')
- new_ada: float32 [1152, 6912], P(None, 'shard')
- bias_update: float32 [16128], replicated
- new_m_qkv: float32 [1152, 3456], P('shard', 'rep')
- new_m_proj: float32 [1152, 1152], P('shard', 'rep')
- new_m_fc1: float32 [1152, 4608], P('shard', 'rep')
- new_m_fc2: float32 [4608, 1152], P('shard', 'rep')
- new_m_ada: float32 [1152, 6912], P('rep', 'shard')
- new_m_bias: float32 [16128], replicated
- new_v_qkv: float32 [1152, 3456], P('shard', 'rep')
- new_v_proj: float32 [1152, 1152], P('shard', 'rep')
- new_v_fc1: float32 [1152, 4608], P('shard', 'rep')
- new_v_fc2: float32 [4608, 1152], P('shard', 'rep')
- new_v_ada: float32 [1152, 6912], P('rep', 'shard')
- new_v_bias: float32 [16128], replicated
The draws below stay inside these ranges and needn't reach their ends.
All inputs are finite; a program needn't handle non-finite values.
Results may differ from the reference program's by a relative error of at most 0.014.
Values may be sent and summed in bfloat16 or wider, within the bound.
No kernel may reach another device: no remote copies, remote signals or barrier semaphores. Data moves between devices by JAX's collectives and lax.ppermute only.
A program may use at most 256 MiB of HBM per device.

```python
import math
import jax
import jax.numpy as jnp
from jax import lax

D = 1152
HD = 72
H = 16
FF = 4608
LEN = 128
LAT_DEV = 1
LATENTS = 32
BIAS_LEN = 16128
PARAMS = 23904000


def draw_latents(key, part):
    normal_part = jax.random.truncated_normal(jax.random.fold_in(key, 11), -5.0, 5.0, (LATENTS, LEN, D), jnp.float32)
    return normal_part.astype(jnp.bfloat16)


def draw_w_qkv(key, part):
    spread_value = D ** (-0.5)
    normal_part = jax.random.truncated_normal(jax.random.fold_in(key, 21), -4.0, 4.0, (D, 3 * H * HD), jnp.float32) * spread_value
    return normal_part


def with_ends(entries, key, smallest, top_value):
    longest = entries.shape.index(max(entries.shape))
    spots = []
    for shift in (0, 1):
        where = [jax.random.randint(jax.random.fold_in(key, axis), (), 0, length) for axis, length in enumerate(entries.shape)]
        where[longest] = (where[longest] + shift) % entries.shape[longest]
        spots.append(tuple(where))
    return entries.at[spots[0]].set(smallest).at[spots[1]].set(top_value)


def shard_levels(own_key, shape, cuts, least, largest):
    factor_of, own = 1.0, jax.random.fold_in(own_key, 6)
    for dim, blocks in cuts:
        draws = jnp.exp(jax.random.uniform(jax.random.fold_in(own, dim), (blocks,), jnp.float32, least / len(cuts), largest / len(cuts)))
        factor_of = factor_of * jnp.repeat(draws, shape[dim] // blocks).reshape([-1 if axis == dim else 1 for axis in range(len(shape))])
    return factor_of


def scatter_about(key, dims, scale, reach, shards=(), kind=jnp.bfloat16):
    entries = jax.random.normal(key, dims, jnp.float32) * scale
    if len(shards) > 0:
        entries = shard_levels(key, dims, shards, -0.22, 0.18) * entries
    return jnp.clip(entries, min=-reach, max=reach).astype(kind)


def setup_inputs(seed: int = 0) -> dict:
    seeds = jax.random.split(jax.random.key(seed), 23)
    latents = draw_latents(jax.random.fold_in(seeds[22], 71), 0)
    cond = scatter_about(seeds[1], (LATENTS, D), 1.0, 6.0, ((0, 32),), jnp.float32)
    timesteps = with_ends(jax.random.randint(seeds[2], (LATENTS,), 0, 1000), jax.random.fold_in(seeds[2], 1), 0, 999).astype(jnp.int32)
    cotangent = scatter_about(seeds[3], (LATENTS, LEN, D), 1.0, 6.0, ((0, 32),))
    w_qkv = draw_w_qkv(jax.random.fold_in(seeds[22], 71), 0)
    w_proj = scatter_about(seeds[5], (H * HD, D), (H * HD // 16) ** -0.5, 0.75, ((0, 16),), jnp.float32)
    w_fc1 = scatter_about(seeds[6], (D, FF), D ** -0.5, 0.1875, ((0, 16),), jnp.float32)
    w_fc2 = scatter_about(seeds[7], (FF, D), (FF // 4) ** -0.5, 0.1875, ((0, 16),), jnp.float32)
    w_ada = scatter_about(seeds[8], (D, 6 * D), (D * LEN) ** -0.5, 0.015625, ((1, 16),), jnp.float32)
    biases = scatter_about(seeds[9], (BIAS_LEN,), 0.5, 3.0, (), jnp.float32)
    m_qkv = scatter_about(seeds[10], (D, 3 * H * HD), (0.1 * PARAMS ** -0.5), 0.00012272017, ((0, 16), (1, 2)), jnp.float32)
    m_proj = scatter_about(seeds[11], (H * HD, D), (0.1 * PARAMS ** -0.5), 0.00012272017, ((0, 16), (1, 2)), jnp.float32)
    m_fc1 = scatter_about(seeds[12], (D, FF), (0.1 * PARAMS ** -0.5), 0.00012272017, ((0, 16), (1, 2)), jnp.float32)
    m_fc2 = scatter_about(seeds[13], (FF, D), (0.1 * PARAMS ** -0.5), 0.00012272017, ((0, 16), (1, 2)), jnp.float32)
    m_ada = scatter_about(seeds[14], (D, 6 * D), (0.1 * PARAMS ** -0.5), 0.00012272017, ((0, 2), (1, 16)), jnp.float32)
    m_bias = scatter_about(seeds[15], (BIAS_LEN,), (0.1 * PARAMS ** -0.5), 0.00012272017, (), jnp.float32)
    v_qkv = jnp.clip(jnp.exp(math.log(1.673360061626994e-10) - 1.3862944 * jax.random.uniform(seeds[16], (D, 3 * H * HD), jnp.float32) ** shard_levels(seeds[16], (D, 3 * H * HD), ((0, 16), (1, 2)), -0.2, 0.2)), 4.183400154067485e-11, 1.673360061626994e-10)
    v_proj = jnp.clip(jnp.exp(math.log(1.673360061626994e-10) - 1.3862944 * jax.random.uniform(seeds[17], (H * HD, D), jnp.float32) ** shard_levels(seeds[17], (H * HD, D), ((0, 16), (1, 2)), -0.2, 0.2)), 4.183400154067485e-11, 1.673360061626994e-10)
    v_fc1 = jnp.clip(jnp.exp(math.log(1.673360061626994e-10) - 1.3862944 * jax.random.uniform(seeds[18], (D, FF), jnp.float32) ** shard_levels(seeds[18], (D, FF), ((0, 16), (1, 2)), -0.2, 0.2)), 4.183400154067485e-11, 1.673360061626994e-10)
    v_fc2 = jnp.clip(jnp.exp(math.log(1.673360061626994e-10) - 1.3862944 * jax.random.uniform(seeds[19], (FF, D), jnp.float32) ** shard_levels(seeds[19], (FF, D), ((0, 16), (1, 2)), -0.2, 0.2)), 4.183400154067485e-11, 1.673360061626994e-10)
    v_ada = jnp.clip(jnp.exp(math.log(1.673360061626994e-10) - 1.3862944 * jax.random.uniform(seeds[20], (D, 6 * D), jnp.float32) ** shard_levels(seeds[20], (D, 6 * D), ((0, 2), (1, 16)), -0.2, 0.2)), 4.183400154067485e-11, 1.673360061626994e-10)
    v_bias = jnp.clip(jnp.exp(jax.random.uniform(seeds[21], (BIAS_LEN,), jnp.float32, math.log(4.183400154067485e-11), math.log(1.673360061626994e-10))), 4.183400154067485e-11, 1.673360061626994e-10)
    return {"latents": latents, "cond": cond, "timesteps": timesteps, "cotangent": cotangent, "w_qkv": w_qkv, "w_proj": w_proj, "w_fc1": w_fc1, "w_fc2": w_fc2, "w_ada": w_ada, "biases": biases, "m_qkv": m_qkv, "m_proj": m_proj, "m_fc1": m_fc1, "m_fc2": m_fc2, "m_ada": m_ada, "m_bias": m_bias, "v_qkv": v_qkv, "v_proj": v_proj, "v_fc1": v_fc1, "v_fc2": v_fc2, "v_ada": v_ada, "v_bias": v_bias}


ln_eps = 1e-06
beta_one = 0.9
beta_two = 0.999
adam_eps = 1e-08
learn_rate = 0.03
decay_rate = 0.01
step_count = 2
gelu_coef = 0.044715

def product(form, left, right):
    return jnp.einsum(form, left.astype(jnp.float32), right.astype(jnp.float32))

def normalize(rows):
    center = rows - lax.optimization_barrier(jnp.mean(rows, axis=-1, keepdims=True))
    rstd = lax.rsqrt(lax.optimization_barrier(jnp.mean(center * center, axis=-1, keepdims=True)) + ln_eps)
    return (center * rstd, rstd)

def norm_back(grad, normed, rstd):
    return rstd * (grad - lax.optimization_barrier(jnp.mean(grad, axis=-1, keepdims=True)) - normed * lax.optimization_barrier(jnp.mean(grad * normed, axis=-1, keepdims=True)))

def gelu_parts(pre):
    root = math.sqrt(2.0 / math.pi)
    inner = root * (pre + gelu_coef * pre * pre * pre)
    tangent = jnp.tanh(inner)
    value = 0.5 * pre * (1.0 + tangent)
    slope = 0.5 * (1.0 + tangent) + 0.5 * pre * (1.0 - tangent * tangent) * root * (1.0 + 3.0 * gelu_coef * pre * pre)
    return (value, slope)

def time_embed(steps, width):
    half = width // 2
    freqs = jnp.exp(-math.log(10000.0) * jnp.arange(half, dtype=jnp.float32) / half)
    angles = steps.astype(jnp.float32)[:, None] * freqs[None, :]
    return jnp.concatenate([jnp.cos(angles), jnp.sin(angles)], axis=1)

def round_partial(term):
    return lax.optimization_barrier(term.astype(jnp.bfloat16)).astype(jnp.float32)

def block_pass(inputs, cotan, mod, wq_b, wp_b, w1_b, w2_b, biases):
    batch, length, width = inputs.shape
    inner = H * HD
    b_q = biases[0:inner]
    b_v = biases[inner:2 * inner]
    b_proj = biases[2 * inner:2 * inner + width]
    b_fc1 = biases[2 * inner + width:2 * inner + width + FF]
    b_fc2 = biases[2 * inner + width + FF:2 * inner + 2 * width + FF]
    parts = [mod[:, i * width:(i + 1) * width][:, None, :] for i in range(6)]
    shift1, scale1, gate1, shift2, scale2, gate2 = parts
    rows = inputs.astype(jnp.float32)
    n_one, r_one = normalize(rows)
    a_one = (n_one * (1.0 + scale1) + shift1).astype(jnp.bfloat16)
    qkv = product('bld,de->ble', a_one, wq_b)
    queries = (qkv[..., :inner] + b_q).astype(jnp.bfloat16).reshape(batch, length, H, HD)
    key_rows = qkv[..., inner:2 * inner].astype(jnp.bfloat16).reshape(batch, length, H, HD)
    value_rows = (qkv[..., 2 * inner:] + b_v).astype(jnp.bfloat16).reshape(batch, length, H, HD)
    factor = HD ** (-0.5)
    scores = product('bqhd,bkhd->bhqk', queries, key_rows) * factor
    top = lax.optimization_barrier(jnp.max(scores, axis=-1, keepdims=True))
    expo = jnp.exp(scores - top)
    probs = expo / lax.optimization_barrier(jnp.sum(expo, axis=-1, keepdims=True))
    probs_b = probs.astype(jnp.bfloat16)
    heads_out = product('bhqk,bkhd->bqhd', probs_b, value_rows).astype(jnp.bfloat16)
    heads_flat = heads_out.reshape(batch, length, inner)
    attn = product('ble,ed->bld', heads_flat, wp_b) + b_proj
    x_one = rows + gate1 * attn
    n_two, r_two = normalize(x_one)
    a_two = (n_two * (1.0 + scale2) + shift2).astype(jnp.bfloat16)
    pre = product('bld,df->blf', a_two, w1_b) + b_fc1
    act_val, act_slope = gelu_parts(pre)
    act = act_val.astype(jnp.bfloat16)
    mlp = product('blf,fd->bld', act, w2_b) + b_fc2
    out = x_one + gate2 * mlp
    grad_out = cotan.astype(jnp.float32)
    d_gate2 = lax.optimization_barrier(jnp.sum(grad_out * mlp, axis=1))
    d_mlp = grad_out * gate2
    d_mlp_b = d_mlp.astype(jnp.bfloat16)
    g_fc2 = product('blf,bld->fd', act, d_mlp_b)
    g_b_fc2 = lax.optimization_barrier(jnp.sum(d_mlp, axis=(0, 1)))
    d_pre = product('bld,fd->blf', d_mlp_b, w2_b) * act_slope
    d_pre_b = d_pre.astype(jnp.bfloat16)
    g_fc1 = product('bld,blf->df', a_two, d_pre_b)
    g_b_fc1 = lax.optimization_barrier(jnp.sum(d_pre, axis=(0, 1)))
    d_a2 = product('blf,df->bld', d_pre_b, w1_b)
    d_shift2 = lax.optimization_barrier(jnp.sum(d_a2, axis=1))
    d_scale2 = lax.optimization_barrier(jnp.sum(d_a2 * n_two, axis=1))
    dx_one = grad_out + norm_back(d_a2 * (1.0 + scale2), n_two, r_two)
    d_gate1 = lax.optimization_barrier(jnp.sum(dx_one * attn, axis=1))
    d_attn = dx_one * gate1
    d_attn_b = d_attn.astype(jnp.bfloat16)
    g_proj = product('ble,bld->ed', heads_flat, d_attn_b)
    g_b_proj = lax.optimization_barrier(jnp.sum(d_attn, axis=(0, 1)))
    d_heads = product('bld,ed->ble', d_attn_b, wp_b).astype(jnp.bfloat16).reshape(batch, length, H, HD)
    delta = lax.optimization_barrier(jnp.sum(d_heads.astype(jnp.float32) * heads_out.astype(jnp.float32), axis=-1))
    delta = jnp.transpose(delta, (0, 2, 1))[..., None]
    d_probs = product('bqhd,bkhd->bhqk', d_heads, value_rows)
    d_scores = (probs * (d_probs - delta) * factor).astype(jnp.bfloat16)
    d_q = product('bhqk,bkhd->bqhd', d_scores, key_rows)
    d_k = product('bhqk,bqhd->bkhd', d_scores, queries)
    d_v = product('bhqk,bqhd->bkhd', probs_b, d_heads)
    g_b_q = lax.optimization_barrier(jnp.sum(d_q, axis=(0, 1))).reshape(inner)
    g_b_v = lax.optimization_barrier(jnp.sum(d_v, axis=(0, 1))).reshape(inner)
    d_qkv = jnp.concatenate([d_q.reshape(batch, length, inner), d_k.reshape(batch, length, inner), d_v.reshape(batch, length, inner)], axis=-1).astype(jnp.bfloat16)
    g_qkv = product('bld,ble->de', a_one, d_qkv)
    d_a1 = product('ble,de->bld', d_qkv, wq_b)
    d_shift1 = lax.optimization_barrier(jnp.sum(d_a1, axis=1))
    d_scale1 = lax.optimization_barrier(jnp.sum(d_a1 * n_one, axis=1))
    d_input = dx_one + norm_back(d_a1 * (1.0 + scale1), n_one, r_one)
    d_mod = jnp.concatenate([d_shift1, d_scale1, d_gate1, d_shift2, d_scale2, d_gate2], axis=1)
    bias_grad = jnp.concatenate([g_b_q, g_b_v, g_b_proj, g_b_fc1, g_b_fc2])
    return (out, d_input, d_mod, (g_qkv, g_proj, g_fc1, g_fc2), bias_grad)

def adam_change(weight, grad, first, second, clip):
    scaled = grad * clip
    first_new = beta_one * first + (1.0 - beta_one) * scaled
    second_new = beta_two * second + (1.0 - beta_two) * scaled * scaled
    first_hat = first_new / (1.0 - beta_one ** step_count)
    second_hat = second_new / (1.0 - beta_two ** step_count)
    change = -learn_rate * (first_hat / (jnp.sqrt(second_hat) + adam_eps) + decay_rate * weight)
    return (change, first_new, second_new)

def adam_step(weight, grad, first, second, clip):
    change, first_new, second_new = adam_change(weight, grad, first, second, clip)
    return (weight + change, first_new, second_new)

def reference(latents, cond, timesteps, cotangent, w_qkv, w_proj, w_fc1, w_fc2, w_ada, biases, m_qkv, m_proj, m_fc1, m_fc2, m_ada, m_bias, v_qkv, v_proj, v_fc1, v_fc2, v_ada, v_bias):
    wq_b = w_qkv.astype(jnp.bfloat16)
    wp_b = w_proj.astype(jnp.bfloat16)
    w1_b = w_fc1.astype(jnp.bfloat16)
    w2_b = w_fc2.astype(jnp.bfloat16)
    wa_b = w_ada.astype(jnp.bfloat16)
    b_ada = biases[BIAS_LEN - 6 * D:]
    cvec = cond + time_embed(timesteps, D)
    silu_c = jax.nn.silu(cvec).astype(jnp.bfloat16)
    mod = jnp.dot(silu_c, wa_b, preferred_element_type=jnp.float32) + b_ada
    run_count = LATENTS // LAT_DEV
    items = (latents.reshape(run_count, LAT_DEV, LEN, D), cotangent.reshape(run_count, LAT_DEV, LEN, D), mod.reshape(run_count, LAT_DEV, 6 * D))

    def scan_step(carry, item):
        out, d_input, d_mod, grads, bias_grad = block_pass(item[0], item[1], item[2], wq_b, wp_b, w1_b, w2_b, biases)
        rounded = tuple((round_partial(g) for g in grads))
        carry = tuple((c + g for c, g in zip(carry, rounded + (bias_grad,))))
        return (carry, (out, d_input, d_mod))
    init = (jnp.zeros((D, 3 * H * HD), jnp.float32), jnp.zeros((H * HD, D), jnp.float32), jnp.zeros((D, FF), jnp.float32), jnp.zeros((FF, D), jnp.float32), jnp.zeros((BIAS_LEN - 6 * D,), jnp.float32))
    sums, (outs, d_inputs, d_mods) = lax.scan(scan_step, init, items)
    g_qkv, g_proj, g_fc1, g_fc2, g_bias_head = sums
    d_mod = d_mods.reshape(LATENTS, 6 * D)
    d_mod_b = d_mod.astype(jnp.bfloat16)
    g_ada = jnp.dot(silu_c.T, d_mod_b, preferred_element_type=jnp.float32)
    g_bias = jnp.concatenate([g_bias_head, lax.optimization_barrier(jnp.sum(d_mod, axis=0))])
    sig = jax.nn.sigmoid(cvec)
    cond_grad = jnp.dot(d_mod_b, wa_b.T, preferred_element_type=jnp.float32) * sig * (1.0 + cvec * (1.0 - sig))
    grads = (g_qkv, g_proj, g_fc1, g_fc2, g_ada, g_bias)
    squares = sum((jnp.sum(g * g) for g in grads))
    gnorm = jnp.sqrt(squares)
    clip = 1.0 / jnp.maximum(gnorm, 1.0)
    weights = (w_qkv, w_proj, w_fc1, w_fc2, w_ada)
    firsts = (m_qkv, m_proj, m_fc1, m_fc2, m_ada)
    seconds = (v_qkv, v_proj, v_fc1, v_fc2, v_ada)
    results = [adam_step(w, g, m, v, clip) for w, g, m, v in zip(weights, grads[:5], firsts, seconds)]
    bias_update, new_m_bias, new_v_bias = adam_change(biases, g_bias, m_bias, v_bias, clip)
    new_w = tuple((r[0] for r in results))
    new_m = tuple((r[1] for r in results))
    new_v = tuple((r[2] for r in results))
    block_out = outs.reshape(LATENTS, LEN, D)
    latents_grad = d_inputs.reshape(LATENTS, LEN, D)
    return (block_out, latents_grad, cond_grad, new_w[0], new_w[1], new_w[2], new_w[3], new_w[4], bias_update, new_m[0], new_m[1], new_m[2], new_m[3], new_m[4], new_m_bias, new_v[0], new_v[1], new_v[2], new_v[3], new_v[4], new_v_bias)
```

```python
import math

import jax
import jax.numpy as jnp
from jax import lax
from jax.sharding import PartitionSpec as P

HD = 72
H = 16
FF = 4608


ln_eps = 1e-06
beta_one = 0.9
beta_two = 0.999
adam_eps = 1e-08
learn_rate = 0.03
decay_rate = 0.01
step_count = 2
gelu_coef = 0.044715


def product(form, left, right):
    return jnp.einsum(form, left, right, preferred_element_type=jnp.float32)


def normalize(rows):
    center = rows - jnp.mean(rows, axis=-1, keepdims=True)
    rstd = lax.rsqrt(jnp.mean(center * center, axis=-1, keepdims=True) + ln_eps)
    return (center * rstd, rstd)


def norm_back(grad, normed, rstd):
    return rstd * (
        grad
        - jnp.mean(grad, axis=-1, keepdims=True)
        - normed * jnp.mean(grad * normed, axis=-1, keepdims=True)
    )


def gelu_parts(pre):
    root = math.sqrt(2.0 / math.pi)
    inner = root * (pre + gelu_coef * pre * pre * pre)
    tangent = jnp.tanh(inner)
    value = 0.5 * pre * (1.0 + tangent)
    slope = 0.5 * (1.0 + tangent) + 0.5 * pre * (1.0 - tangent * tangent) * root * (
        1.0 + 3.0 * gelu_coef * pre * pre
    )
    return (value, slope)


def time_embed(steps, width):
    half = width // 2
    freqs = jnp.exp(-math.log(10000.0) * jnp.arange(half, dtype=jnp.float32) / half)
    angles = steps.astype(jnp.float32)[:, None] * freqs[None, :]
    return jnp.concatenate([jnp.cos(angles), jnp.sin(angles)], axis=1)


def adam_change(weight, grad, first, second, clip):
    scaled = grad * clip
    first_new = beta_one * first + (1.0 - beta_one) * scaled
    second_new = beta_two * second + (1.0 - beta_two) * scaled * scaled
    first_hat = first_new / (1.0 - beta_one**step_count)
    second_hat = second_new / (1.0 - beta_two**step_count)
    change = -learn_rate * (first_hat / (jnp.sqrt(second_hat) + adam_eps) + decay_rate * weight)
    return (change, first_new, second_new)


def shards(
    latents,
    cond,
    timesteps,
    cotangent,
    w_qkv,
    w_proj,
    w_fc1,
    w_fc2,
    w_ada,
    biases,
    m_qkv,
    m_proj,
    m_fc1,
    m_fc2,
    m_ada,
    m_bias,
    v_qkv,
    v_proj,
    v_fc1,
    v_fc2,
    v_ada,
    v_bias,
):
    axes = ("rep", "shard")
    replicas = lax.axis_size("rep")
    parts = lax.axis_size("shard")
    devices = replicas * parts
    rank = lax.axis_index("rep")
    turn = rank % 2
    couples = [(i, i ^ 1) for i in range(replicas)]
    length, width = latents.shape[1:]
    inner = H * HD
    half = inner // 2
    heads = H // 2
    rows = w_qkv.shape[0]
    folds = FF // (2 * width)
    unit = FF // (2 * parts * folds)

    def swap(value):
        return lax.ppermute(value, "rep", couples)

    def ordered(own, other, axis):
        first = jnp.concatenate([own, other], axis=axis)
        second = jnp.concatenate([other, own], axis=axis)
        return jnp.where(turn == 0, first, second)

    def own_half(value, axis):
        count = value.shape[axis] // 2
        return lax.dynamic_slice_in_dim(value, turn * count, count, axis)

    def spread(value):
        copies = jnp.broadcast_to(value, (devices,) + value.shape[1:])
        return lax.all_to_all(copies, axes, split_axis=0, concat_axis=0, tiled=True)

    b_q = own_half(biases[0:inner], 0)
    b_v = own_half(biases[inner : 2 * inner], 0)
    b_proj = biases[2 * inner : 2 * inner + width]
    b_fc1 = biases[2 * inner + width : 2 * inner + width + FF]
    b_fc2 = biases[2 * inner + width + FF : 2 * inner + 2 * width + FF]
    b_ada = biases[biases.shape[0] - 6 * width :]
    units = lax.dynamic_index_in_dim(
        b_fc1.reshape(parts, 2, folds, unit), turn, 1, keepdims=False
    )
    b_one = jnp.transpose(units, (1, 0, 2)).reshape(folds, width)

    wq_half = own_half(w_qkv.astype(jnp.bfloat16).reshape(rows, 3, inner), 2)
    pack_attn = jnp.concatenate(
        [w_proj.astype(jnp.bfloat16), wq_half.reshape(rows, 3 * half)], axis=1
    )
    full_attn = lax.all_gather(pack_attn, "shard", axis=0, tiled=True)
    wp_b = full_attn[:, :width]
    wq_b = full_attn[:, width:]
    w1_half = lax.dynamic_index_in_dim(
        w_fc1.astype(jnp.bfloat16).reshape(rows, parts, 2, folds, unit), turn, 2, keepdims=False
    )
    w1_half = jnp.transpose(w1_half, (0, 2, 1, 3)).reshape(rows, folds * width)
    w2_half = own_half(w_fc2.astype(jnp.bfloat16), 0).reshape(folds, rows, width)
    pack_mlp = jnp.concatenate([w1_half] + [w2_half[f] for f in range(folds)], axis=1)
    full_mlp = lax.all_gather(pack_mlp, "shard", axis=0, tiled=True)
    w1_b = [full_mlp[:, f * width : (f + 1) * width] for f in range(folds)]
    w2_b = [full_mlp[:, (folds + f) * width : (folds + f + 1) * width] for f in range(folds)]

    cvec = cond + time_embed(timesteps, width)
    silu_c = jax.nn.silu(cvec).astype(jnp.bfloat16)
    ada_local = w_ada.astype(jnp.bfloat16)
    silu_all = spread(silu_c)
    silu_group = lax.dynamic_slice_in_dim(silu_all, rank * parts, parts, 0)
    mod_cols = jnp.dot(silu_group, ada_local, preferred_element_type=jnp.float32)
    mod = lax.all_to_all(mod_cols, "shard", split_axis=0, concat_axis=1, tiled=True) + b_ada
    shift1, scale1, gate1, shift2, scale2, gate2 = [
        mod[:, i * width : (i + 1) * width] for i in range(6)
    ]

    tokens = latents[0].astype(jnp.float32)
    n_one, r_one = normalize(tokens)
    a_one = (n_one * (1.0 + scale1) + shift1).astype(jnp.bfloat16)
    grad_out = cotangent[0].astype(jnp.float32)
    d_mlp = grad_out * gate2
    d_mlp_b = d_mlp.astype(jnp.bfloat16)
    a_one2 = jnp.concatenate([a_one, swap(a_one)], axis=0)
    d_mlp2 = jnp.concatenate([d_mlp_b, swap(d_mlp_b)], axis=0)

    qkv = product("ld,de->le", a_one2, wq_b)
    shape = (2, length, heads, HD)
    queries = (qkv[:, :half] + b_q).astype(jnp.bfloat16).reshape(shape)
    key_rows = qkv[:, half : 2 * half].astype(jnp.bfloat16).reshape(shape)
    value_rows = (qkv[:, 2 * half :] + b_v).astype(jnp.bfloat16).reshape(shape)
    factor = HD ** (-0.5)
    scores = product("bqhd,bkhd->bhqk", queries, key_rows) * factor
    top = jnp.max(scores, axis=-1, keepdims=True)
    expo = jnp.exp(scores - top)
    probs = expo / jnp.sum(expo, axis=-1, keepdims=True)
    probs_b = probs.astype(jnp.bfloat16)
    heads_out = product("bhqk,bkhd->bqhd", probs_b, value_rows).astype(jnp.bfloat16)
    heads_flat = heads_out.reshape(2, length, half)
    heads_other = swap(heads_flat)[::-1]
    heads_own = ordered(heads_flat[0], heads_other[0], 1)
    attn = product("le,ed->ld", heads_own, wp_b) + b_proj
    x_one = tokens + gate1 * attn
    n_two, r_two = normalize(x_one)
    a_two = (n_two * (1.0 + scale2) + shift2).astype(jnp.bfloat16)
    a_two2 = jnp.concatenate([a_two, swap(a_two)], axis=0)

    mlp_sum = 0.0
    d_a2_sum = 0.0
    g_one = []
    g_two = []
    g_b_one = []
    for f in range(folds):
        pre = product("ld,df->lf", a_two2, w1_b[f]) + b_one[f]
        act_val, act_slope = gelu_parts(pre)
        act = act_val.astype(jnp.bfloat16)
        mlp_sum = mlp_sum + product("lf,fd->ld", act, w2_b[f])
        d_pre = product("ld,fd->lf", d_mlp2, w2_b[f]) * act_slope
        d_pre_b = d_pre.astype(jnp.bfloat16)
        d_a2_sum = d_a2_sum + product("lf,df->ld", d_pre_b, w1_b[f])
        g_one.append(product("ld,lf->df", a_two2, d_pre_b).astype(jnp.bfloat16))
        g_two.append(product("lf,ld->fd", act, d_mlp2).astype(jnp.bfloat16))
        g_b_one.append(jnp.sum(d_pre, axis=0))
    grads_mlp = lax.psum_scatter(
        jnp.concatenate(g_one + g_two, axis=1), "shard", scatter_dimension=0, tiled=True
    )
    d_a2 = d_a2_sum[:length] + swap(d_a2_sum[length:].astype(jnp.bfloat16)).astype(jnp.float32)
    mlp = (
        mlp_sum[:length]
        + swap(mlp_sum[length:].astype(jnp.bfloat16)).astype(jnp.float32)
        + b_fc2
    )
    block_out = (x_one + gate2 * mlp)[None]
    d_gate2 = jnp.sum(grad_out * mlp, axis=0)
    g_b_fc2 = jnp.sum(d_mlp, axis=0)

    d_shift2 = jnp.sum(d_a2, axis=0)
    d_scale2 = jnp.sum(d_a2 * n_two, axis=0)
    dx_one = grad_out + norm_back(d_a2 * (1.0 + scale2), n_two, r_two)
    d_gate1 = jnp.sum(dx_one * attn, axis=0)
    d_attn = dx_one * gate1
    d_attn_b = d_attn.astype(jnp.bfloat16)
    g_b_proj = jnp.sum(d_attn, axis=0)
    d_attn2 = jnp.concatenate([d_attn_b, swap(d_attn_b)], axis=0)
    d_heads = (
        product("ld,ed->le", d_attn2, own_half(wp_b, 0)).astype(jnp.bfloat16).reshape(shape)
    )
    heads_all = jnp.concatenate(
        [heads_own, ordered(heads_flat[1], heads_other[1], 1)], axis=0
    )
    g_proj = product("le,ld->ed", heads_all, own_half(d_attn2, 1)).astype(jnp.bfloat16)
    delta = jnp.sum(d_heads.astype(jnp.float32) * heads_out.astype(jnp.float32), axis=-1)
    delta = jnp.transpose(delta, (0, 2, 1))[..., None]
    d_probs = product("bqhd,bkhd->bhqk", d_heads, value_rows)
    d_scores = (probs * (d_probs - delta) * factor).astype(jnp.bfloat16)
    d_q = product("bhqk,bkhd->bqhd", d_scores, key_rows)
    d_k = product("bhqk,bqhd->bkhd", d_scores, queries)
    d_v = product("bhqk,bqhd->bkhd", probs_b, d_heads)
    g_b_q = jnp.sum(d_q, axis=(0, 1)).reshape(half)
    g_b_v = jnp.sum(d_v, axis=(0, 1)).reshape(half)
    d_qkv = jnp.concatenate(
        [piece.astype(jnp.bfloat16).reshape(2 * length, half) for piece in (d_q, d_k, d_v)],
        axis=1,
    )
    g_qkv = product("ld,le->de", a_one2, d_qkv).astype(jnp.bfloat16)
    grads_attn = lax.psum_scatter(
        jnp.concatenate([g_proj, g_qkv], axis=1), "shard", scatter_dimension=0, tiled=True
    )
    d_a1_sum = product("le,de->ld", d_qkv, wq_b)
    d_a1 = d_a1_sum[:length] + swap(d_a1_sum[length:].astype(jnp.bfloat16)).astype(jnp.float32)
    d_shift1 = jnp.sum(d_a1, axis=0)
    d_scale1 = jnp.sum(d_a1 * n_one, axis=0)
    latents_grad = (dx_one + norm_back(d_a1 * (1.0 + scale1), n_one, r_one))[None]

    d_mod = jnp.concatenate([d_shift1, d_scale1, d_gate1, d_shift2, d_scale2, d_gate2])
    d_mod_b = d_mod.astype(jnp.bfloat16).reshape(1, parts, d_mod.shape[0] // parts)
    d_mod_b = jnp.broadcast_to(d_mod_b, (replicas,) + d_mod_b.shape[1:])
    d_mod_cols = lax.all_to_all(
        d_mod_b.reshape(devices, d_mod_b.shape[2]), axes, split_axis=0, concat_axis=0, tiled=True
    )
    g_ada = jnp.dot(silu_all.T, d_mod_cols, preferred_element_type=jnp.float32)
    group_cols = lax.dynamic_slice_in_dim(d_mod_cols, rank * parts, parts, 0)
    silu_terms = jnp.dot(group_cols, ada_local.T, preferred_element_type=jnp.float32)
    silu_terms = lax.all_to_all(silu_terms, "shard", split_axis=0, concat_axis=0, tiled=True)
    silu_grad = jnp.sum(silu_terms, axis=0, keepdims=True)
    sig = jax.nn.sigmoid(cvec)
    cond_grad = silu_grad * sig * (1.0 + cvec * (1.0 - sig))

    mine = jnp.arange(2) == turn
    units_one = jnp.transpose(jnp.stack(g_b_one).reshape(folds, parts, unit), (1, 0, 2))
    bias_partial = jnp.concatenate(
        [
            jnp.where(mine[:, None], g_b_q[None], 0.0).reshape(inner),
            jnp.where(mine[:, None], g_b_v[None], 0.0).reshape(inner),
            g_b_proj,
            jnp.where(mine[None, :, None, None], units_one[:, None], 0.0).reshape(FF),
            g_b_fc2,
            d_mod,
        ]
    )
    chunk = bias_partial.shape[0] // devices
    bias_terms = lax.all_to_all(
        bias_partial.reshape(devices, chunk), axes, split_axis=0, concat_axis=0, tiled=True
    )
    bias_chunk = jnp.sum(bias_terms, axis=0)

    def complete(own):
        return swap(own) if replicas == 2 else jnp.zeros_like(own)

    def share(own, axis):
        if replicas == 2:
            return own
        return lax.psum_scatter(
            own.astype(jnp.float32), "rep", scatter_dimension=axis, tiled=True
        )

    def split(value):
        if replicas == 2:
            return own_half(value, 1)
        return share(value, 1)

    own_proj = grads_attn[:, :half]
    if replicas > 2:
        own_proj = share(ordered(own_proj, jnp.zeros_like(own_proj), 1), 1)
    own_qkv = grads_attn[:, half:].reshape(rows, 3, half)
    full_qkv = ordered(own_qkv, complete(own_qkv), 2).reshape(rows, 3 * inner)
    own_mlp = grads_mlp[:, None]
    full_mlp_grad = ordered(own_mlp, complete(own_mlp), 1)
    full_one = full_mlp_grad[:, :, : folds * width].reshape(rows, 2, folds, parts, unit)
    full_one = jnp.transpose(full_one, (0, 3, 1, 2, 4)).reshape(rows, FF)
    full_two = full_mlp_grad[:, :, folds * width :].reshape(rows, 2, folds, width)
    full_two = jnp.transpose(full_two, (1, 2, 0, 3)).reshape(2 * folds * rows, width)
    count_ada = width // replicas
    own_ada = lax.dynamic_slice_in_dim(g_ada, rank * count_ada, count_ada, 0)
    pieces = [split(full_qkv), own_proj, split(full_one), split(full_two), own_ada]
    pieces = [piece.astype(jnp.float32) for piece in pieces]
    if replicas == 2:
        counted = [grads_attn.astype(jnp.float32), grads_mlp.astype(jnp.float32), own_ada]
    else:
        counted = pieces
    squares = sum((jnp.sum(p * p) for p in counted)) + jnp.sum(bias_chunk * bias_chunk)
    totals = spread(jnp.concatenate([bias_chunk, squares[None]])[None])
    g_bias = totals[:, :chunk].reshape(devices * chunk)
    gnorm = jnp.sqrt(jnp.sum(totals[:, chunk]))
    clip = 1.0 / jnp.maximum(gnorm, 1.0)

    weights = (w_qkv, w_proj, w_fc1, w_fc2, w_ada)
    dims = (1, 1, 1, 1, 0)
    firsts = (m_qkv, m_proj, m_fc1, m_fc2, m_ada)
    seconds = (v_qkv, v_proj, v_fc1, v_fc2, v_ada)
    new_w = []
    new_m = []
    new_v = []
    for weight, dim, grad, first, second in zip(weights, dims, pieces, firsts, seconds):
        count = weight.shape[dim] // replicas
        own = lax.dynamic_slice_in_dim(weight, rank * count, count, dim)
        change, first_new, second_new = adam_change(own, grad, first, second, clip)
        change = change.astype(jnp.bfloat16)
        if replicas == 2:
            changes = ordered(change, swap(change), dim)
        else:
            changes = lax.all_gather(change, "rep", axis=dim, tiled=True)
        new_w.append(weight + changes.astype(jnp.float32))
        new_m.append(first_new)
        new_v.append(second_new)
    bias_update, new_m_bias, new_v_bias = adam_change(biases, g_bias, m_bias, v_bias, clip)
    return (
        block_out,
        latents_grad,
        cond_grad,
        *new_w,
        bias_update,
        *new_m,
        new_m_bias,
        *new_v,
        new_v_bias,
    )


def solution(mesh):
    in_specs = (
        P(("rep", "shard"), None, None),
        P(("rep", "shard"), None),
        P(("rep", "shard")),
        P(("rep", "shard"), None, None),
        P("shard", None),
        P("shard", None),
        P("shard", None),
        P("shard", None),
        P(None, "shard"),
        P(),
        P("shard", "rep"),
        P("shard", "rep"),
        P("shard", "rep"),
        P("shard", "rep"),
        P("rep", "shard"),
        P(),
        P("shard", "rep"),
        P("shard", "rep"),
        P("shard", "rep"),
        P("shard", "rep"),
        P("rep", "shard"),
        P(),
    )
    out_specs = (
        P(("rep", "shard"), None, None),
        P(("rep", "shard"), None, None),
        P(("rep", "shard"), None),
        P("shard", None),
        P("shard", None),
        P("shard", None),
        P("shard", None),
        P(None, "shard"),
        P(),
        P("shard", "rep"),
        P("shard", "rep"),
        P("shard", "rep"),
        P("shard", "rep"),
        P("rep", "shard"),
        P(),
        P("shard", "rep"),
        P("shard", "rep"),
        P("shard", "rep"),
        P("shard", "rep"),
        P("rep", "shard"),
        P(),
    )
    return jax.shard_map(shards, mesh=mesh, in_specs=in_specs, out_specs=out_specs, check_vma=False)
```

```python
import math

import jax
import jax.numpy as jnp
from jax import lax
from jax.experimental import pallas as pl
from jax.experimental.pallas import tpu as pltpu
from jax.sharding import PartitionSpec as P

HD = 72
H = 16
FF = 4608


ln_eps = 1e-06
beta_one = 0.9
beta_two = 0.999
adam_eps = 1e-08
learn_rate = 0.03
decay_rate = 0.01
step_count = 2
gelu_coef = 0.044715


def product(form, left, right):
    return jnp.einsum(form, left, right, preferred_element_type=jnp.float32)


def normalize(rows):
    center = rows - jnp.mean(rows, axis=-1, keepdims=True)
    rstd = lax.rsqrt(jnp.mean(center * center, axis=-1, keepdims=True) + ln_eps)
    return (center * rstd, rstd)


def norm_back(grad, normed, rstd):
    return rstd * (
        grad
        - jnp.mean(grad, axis=-1, keepdims=True)
        - normed * jnp.mean(grad * normed, axis=-1, keepdims=True)
    )


def gelu_parts(pre):
    root = math.sqrt(2.0 / math.pi)
    inner = root * (pre + gelu_coef * pre * pre * pre)
    tangent = jnp.tanh(inner)
    value = 0.5 * pre * (1.0 + tangent)
    slope = 0.5 * (1.0 + tangent) + 0.5 * pre * (1.0 - tangent * tangent) * root * (
        1.0 + 3.0 * gelu_coef * pre * pre
    )
    return (value, slope)


def time_embed(steps, width):
    half = width // 2
    freqs = jnp.exp(-math.log(10000.0) * jnp.arange(half, dtype=jnp.float32) / half)
    angles = steps.astype(jnp.float32)[:, None] * freqs[None, :]
    return jnp.concatenate([jnp.cos(angles), jnp.sin(angles)], axis=1)


def adam_change(weight, grad, first, second, clip):
    scaled = grad * clip
    first_new = beta_one * first + (1.0 - beta_one) * scaled
    second_new = beta_two * second + (1.0 - beta_two) * scaled * scaled
    first_hat = first_new / (1.0 - beta_one**step_count)
    second_hat = second_new / (1.0 - beta_two**step_count)
    change = -learn_rate * (first_hat / (jnp.sqrt(second_hat) + adam_eps) + decay_rate * weight)
    return (change, first_new, second_new)


def outer(left, right):
    return lax.dot_general(
        left, right, (((0,), (0,)), ((), ())), preferred_element_type=jnp.float32
    ).astype(jnp.bfloat16)


def pack_products(pairs, picks, starts, total, block):
    lefts, rights = pairs
    tall, width = lefts[0].shape
    wide = total // len(picks)

    def body(*refs):
        step = pl.program_id(0)
        out = refs[-1]
        for j, writes in enumerate(picks):

            @pl.when(step == j)
            def _():
                for left, right, column in writes:
                    value = outer(refs[left][...], refs[len(lefts) + right][...])
                    out[:, column : column + value.shape[1]] = value

    return pl.pallas_call(
        body,
        grid=(len(picks), width // block),
        in_specs=[pl.BlockSpec((tall, block), lambda j, i: (0, i)) for _ in lefts]
        + [pl.BlockSpec(r.shape, lambda j, i: (0, 0)) for r in rights],
        out_specs=pl.BlockSpec((block, wide), lambda j, i: (i, j)),
        out_shape=jax.ShapeDtypeStruct((width, total), jnp.bfloat16),
        name=starts,
    )(*lefts, *rights)


def update_both(weight, grads, first, second, first_far, second_far, scalars, plan):
    size, blocks = plan
    clip, turn = scalars

    def cut(ref, start):
        return ref[:, start : start + size]

    def put(ref, start, value):
        ref[:, start : start + size] = value

    def body(clip_ref, turn_ref, w_ref, *refs):
        g_refs = refs[: len(grads)]
        m_ref, v_ref, mf_ref, vf_ref, w_out, m_out, v_out = refs[len(grads) :]
        scale = clip_ref[0]
        for place in (0, 1):

            @pl.when(turn_ref[0] == place)
            def _():
                for w_at, g_member, g_at, m_member, m_at in blocks:
                    source = g_refs[0] if g_member in (-1, place) else g_refs[1]
                    grad = cut(source, g_at).astype(jnp.float32) * scale
                    own = m_member == place
                    first_old = cut(m_ref if own else mf_ref, m_at)
                    second_old = cut(v_ref if own else vf_ref, m_at)
                    if own:
                        put(m_out, m_at, beta_one * first_old + (1.0 - beta_one) * grad)
                        put(v_out, m_at, beta_two * second_old + (1.0 - beta_two) * grad * grad)
                        first_old = first_old.astype(jnp.bfloat16)
                        second_old = second_old.astype(jnp.bfloat16)
                    first_new = beta_one * first_old.astype(jnp.float32) + (1.0 - beta_one) * grad
                    second_new = (
                        beta_two * second_old.astype(jnp.float32) + (1.0 - beta_two) * grad * grad
                    )
                    first_hat = first_new / (1.0 - beta_one**step_count)
                    second_hat = second_new / (1.0 - beta_two**step_count)
                    old = cut(w_ref, w_at)
                    change = -learn_rate * (
                        first_hat / (jnp.sqrt(second_hat) + adam_eps) + decay_rate * old
                    )
                    put(w_out, w_at, old + change)

    vmem = pl.BlockSpec(memory_space=pltpu.VMEM)
    smem = pl.BlockSpec(memory_space=pltpu.SMEM)
    return pl.pallas_call(
        body,
        in_specs=[smem, smem] + [vmem] * (5 + len(grads)),
        out_specs=[vmem] * 3,
        out_shape=[jax.ShapeDtypeStruct(a.shape, a.dtype) for a in (weight, first, second)],
        name="update",
    )(clip, turn, weight, *grads, first, second, first_far, second_far)


def shards(
    latents,
    cond,
    timesteps,
    cotangent,
    w_qkv,
    w_proj,
    w_fc1,
    w_fc2,
    w_ada,
    biases,
    m_qkv,
    m_proj,
    m_fc1,
    m_fc2,
    m_ada,
    m_bias,
    v_qkv,
    v_proj,
    v_fc1,
    v_fc2,
    v_ada,
    v_bias,
):
    axes = ("rep", "shard")
    replicas = lax.axis_size("rep")
    parts = lax.axis_size("shard")
    devices = replicas * parts
    rank = lax.axis_index("rep")
    turn = rank % 2
    couples = [(i, i ^ 1) for i in range(replicas)]
    length, width = latents.shape[1:]
    inner = H * HD
    half = inner // 2
    heads = H // 2
    rows = w_qkv.shape[0]
    folds = FF // (2 * width)
    unit = FF // (2 * parts * folds)

    def swap(value):
        return lax.ppermute(value, "rep", couples)

    def ordered(own, other, axis):
        first = jnp.concatenate([own, other], axis=axis)
        second = jnp.concatenate([other, own], axis=axis)
        return jnp.where(turn == 0, first, second)

    def own_half(value, axis):
        count = value.shape[axis] // 2
        return lax.dynamic_slice_in_dim(value, turn * count, count, axis)

    def spread(value):
        copies = jnp.broadcast_to(value, (devices,) + value.shape[1:])
        return lax.all_to_all(copies, axes, split_axis=0, concat_axis=0, tiled=True)

    b_q = own_half(biases[0:inner], 0)
    b_v = own_half(biases[inner : 2 * inner], 0)
    b_proj = biases[2 * inner : 2 * inner + width]
    b_fc1 = biases[2 * inner + width : 2 * inner + width + FF]
    b_fc2 = biases[2 * inner + width + FF : 2 * inner + 2 * width + FF]
    b_ada = biases[biases.shape[0] - 6 * width :]
    units = lax.dynamic_index_in_dim(
        b_fc1.reshape(parts, 2, folds, unit), turn, 1, keepdims=False
    )
    b_one = jnp.transpose(units, (1, 0, 2)).reshape(folds, width)

    wq_half = own_half(w_qkv.astype(jnp.bfloat16).reshape(rows, 3, inner), 2)
    pack_attn = jnp.concatenate(
        [w_proj.astype(jnp.bfloat16), wq_half.reshape(rows, 3 * half)], axis=1
    )
    full_attn = lax.all_gather(pack_attn, "shard", axis=0, tiled=True)
    wp_b = full_attn[:, :width]
    wq_b = full_attn[:, width:]
    w1_half = lax.dynamic_index_in_dim(
        w_fc1.astype(jnp.bfloat16).reshape(rows, parts, 2, folds, unit), turn, 2, keepdims=False
    )
    w1_half = jnp.transpose(w1_half, (0, 2, 1, 3)).reshape(rows, folds * width)
    w2_half = own_half(w_fc2.astype(jnp.bfloat16), 0).reshape(folds, rows, width)
    pack_mlp = jnp.concatenate([w1_half] + [w2_half[f] for f in range(folds)], axis=1)
    full_mlp = lax.all_gather(pack_mlp, "shard", axis=0, tiled=True)
    w1_b = [full_mlp[:, f * width : (f + 1) * width] for f in range(folds)]
    w2_b = [full_mlp[:, (folds + f) * width : (folds + f + 1) * width] for f in range(folds)]

    cvec = cond + time_embed(timesteps, width)
    silu_c = jax.nn.silu(cvec).astype(jnp.bfloat16)
    ada_local = w_ada.astype(jnp.bfloat16)
    silu_all = spread(silu_c)
    silu_group = lax.dynamic_slice_in_dim(silu_all, rank * parts, parts, 0)
    mod_cols = jnp.dot(silu_group, ada_local, preferred_element_type=jnp.float32)
    mod = lax.all_to_all(mod_cols, "shard", split_axis=0, concat_axis=1, tiled=True) + b_ada
    shift1, scale1, gate1, shift2, scale2, gate2 = [
        mod[:, i * width : (i + 1) * width] for i in range(6)
    ]

    tokens = latents[0].astype(jnp.float32)
    n_one, r_one = normalize(tokens)
    a_one = (n_one * (1.0 + scale1) + shift1).astype(jnp.bfloat16)
    grad_out = cotangent[0].astype(jnp.float32)
    d_mlp = grad_out * gate2
    d_mlp_b = d_mlp.astype(jnp.bfloat16)
    a_one2 = jnp.concatenate([a_one, swap(a_one)], axis=0)
    d_mlp2 = jnp.concatenate([d_mlp_b, swap(d_mlp_b)], axis=0)

    qkv = product("ld,de->le", a_one2, wq_b)
    shape = (2, length, heads, HD)
    queries = (qkv[:, :half] + b_q).astype(jnp.bfloat16).reshape(shape)
    key_rows = qkv[:, half : 2 * half].astype(jnp.bfloat16).reshape(shape)
    value_rows = (qkv[:, 2 * half :] + b_v).astype(jnp.bfloat16).reshape(shape)
    factor = HD ** (-0.5)
    scores = product("bqhd,bkhd->bhqk", queries, key_rows) * factor
    top = jnp.max(scores, axis=-1, keepdims=True)
    expo = jnp.exp(scores - top)
    probs = expo / jnp.sum(expo, axis=-1, keepdims=True)
    probs_b = probs.astype(jnp.bfloat16)
    heads_out = product("bhqk,bkhd->bqhd", probs_b, value_rows).astype(jnp.bfloat16)
    heads_flat = heads_out.reshape(2, length, half)
    heads_other = swap(heads_flat)[::-1]
    heads_own = ordered(heads_flat[0], heads_other[0], 1)
    attn = product("le,ed->ld", heads_own, wp_b) + b_proj
    x_one = tokens + gate1 * attn
    n_two, r_two = normalize(x_one)
    a_two = (n_two * (1.0 + scale2) + shift2).astype(jnp.bfloat16)
    a_two2 = jnp.concatenate([a_two, swap(a_two)], axis=0)

    g_one = []
    g_two = []
    g_b_one = []
    for f in range(folds):
        pre = product("ld,df->lf", a_two2, w1_b[f]) + b_one[f]
        act_val, act_slope = gelu_parts(pre)
        act = act_val.astype(jnp.bfloat16)
        d_pre = product("ld,fd->lf", d_mlp2, w2_b[f]) * act_slope
        d_pre_b = d_pre.astype(jnp.bfloat16)
        g_one.append(d_pre_b)
        g_two.append(act)
        g_b_one.append(jnp.sum(d_pre, axis=0))
    picks = [[(0, f, 0)] for f in range(folds)] + [[(1 + f, folds, 0)] for f in range(folds)]
    pack_mlp_grad = pack_products(
        ([a_two2] + g_two, g_one + [d_mlp2]), picks, "pack_mlp", 2 * folds * width, width
    )
    g_one, g_two, pack_mlp_grad = lax.optimization_barrier((g_one, g_two, pack_mlp_grad))
    mlp_sum = 0.0
    d_a2_sum = 0.0
    for f in range(folds):
        d_a2_sum = d_a2_sum + product("lf,df->ld", g_one[f], w1_b[f])
        mlp_sum = mlp_sum + product("lf,fd->ld", g_two[f], w2_b[f])
    d_a2_far = swap(d_a2_sum[length:].astype(jnp.bfloat16))
    grads_mlp = lax.psum_scatter(pack_mlp_grad, "shard", scatter_dimension=0, tiled=True)
    d_a2 = d_a2_sum[:length] + d_a2_far.astype(jnp.float32)
    mlp = (
        mlp_sum[:length]
        + swap(mlp_sum[length:].astype(jnp.bfloat16)).astype(jnp.float32)
        + b_fc2
    )
    block_out = (x_one + gate2 * mlp)[None]
    d_gate2 = jnp.sum(grad_out * mlp, axis=0)
    g_b_fc2 = jnp.sum(d_mlp, axis=0)

    d_shift2 = jnp.sum(d_a2, axis=0)
    d_scale2 = jnp.sum(d_a2 * n_two, axis=0)
    dx_one = grad_out + norm_back(d_a2 * (1.0 + scale2), n_two, r_two)
    d_gate1 = jnp.sum(dx_one * attn, axis=0)
    d_attn = dx_one * gate1
    d_attn_b = d_attn.astype(jnp.bfloat16)
    g_b_proj = jnp.sum(d_attn, axis=0)
    d_attn2 = jnp.concatenate([d_attn_b, swap(d_attn_b)], axis=0)
    d_heads = (
        product("ld,ed->le", d_attn2, own_half(wp_b, 0)).astype(jnp.bfloat16).reshape(shape)
    )
    heads_all = jnp.concatenate(
        [heads_own, ordered(heads_flat[1], heads_other[1], 1)], axis=0
    )
    delta = jnp.sum(d_heads.astype(jnp.float32) * heads_out.astype(jnp.float32), axis=-1)
    delta = jnp.transpose(delta, (0, 2, 1))[..., None]
    d_probs = product("bqhd,bkhd->bhqk", d_heads, value_rows)
    d_scores = (probs * (d_probs - delta) * factor).astype(jnp.bfloat16)
    d_q = product("bhqk,bkhd->bqhd", d_scores, key_rows)
    d_k = product("bhqk,bqhd->bkhd", d_scores, queries)
    d_v = product("bhqk,bqhd->bkhd", probs_b, d_heads)
    g_b_q = jnp.sum(d_q, axis=(0, 1)).reshape(half)
    g_b_v = jnp.sum(d_v, axis=(0, 1)).reshape(half)
    d_qkv = jnp.concatenate(
        [piece.astype(jnp.bfloat16).reshape(2 * length, half) for piece in (d_q, d_k, d_v)],
        axis=1,
    )
    proj_wide = -(-half // 128) * 128
    d_attn_half = jnp.pad(own_half(d_attn2, 1), ((0, 0), (0, proj_wide - half)))
    pack_attn_grad = pack_products(
        ([heads_all, a_one2], [d_attn_half, d_qkv]),
        [[(0, 0, 0), (1, 1, proj_wide)]],
        "pack_attn",
        proj_wide + 3 * half,
        3 * 128,
    )
    firsts = (m_qkv, m_proj, m_fc1, m_fc2, m_ada.T)
    seconds = (v_qkv, v_proj, v_fc1, v_fc2, v_ada.T)
    fars = []
    if replicas == 2:
        fars = [swap(value.astype(jnp.bfloat16)) for value in firsts + seconds]
    fars, grads_mlp, pack_attn_grad = lax.optimization_barrier((fars, grads_mlp, pack_attn_grad))
    grads_attn = lax.psum_scatter(pack_attn_grad, "shard", scatter_dimension=0, tiled=True)
    d_a1_sum = product("le,de->ld", d_qkv, wq_b)
    d_a1 = d_a1_sum[:length] + swap(d_a1_sum[length:].astype(jnp.bfloat16)).astype(jnp.float32)
    d_shift1 = jnp.sum(d_a1, axis=0)
    d_scale1 = jnp.sum(d_a1 * n_one, axis=0)
    latents_grad = (dx_one + norm_back(d_a1 * (1.0 + scale1), n_one, r_one))[None]

    d_mod = jnp.concatenate([d_shift1, d_scale1, d_gate1, d_shift2, d_scale2, d_gate2])
    d_mod_b = d_mod.astype(jnp.bfloat16).reshape(1, parts, d_mod.shape[0] // parts)
    d_mod_b = jnp.broadcast_to(d_mod_b, (replicas,) + d_mod_b.shape[1:])
    d_mod_cols = lax.all_to_all(
        d_mod_b.reshape(devices, d_mod_b.shape[2]), axes, split_axis=0, concat_axis=0, tiled=True
    )
    g_ada = jnp.dot(d_mod_cols.T, silu_all, preferred_element_type=jnp.float32)
    group_cols = lax.dynamic_slice_in_dim(d_mod_cols, rank * parts, parts, 0)
    silu_terms = jnp.dot(group_cols, ada_local.T, preferred_element_type=jnp.float32)
    silu_terms = lax.all_to_all(silu_terms, "shard", split_axis=0, concat_axis=0, tiled=True)
    silu_grad = jnp.sum(silu_terms, axis=0, keepdims=True)
    sig = jax.nn.sigmoid(cvec)
    cond_grad = silu_grad * sig * (1.0 + cvec * (1.0 - sig))

    mine = jnp.arange(2) == turn
    units_one = jnp.transpose(jnp.stack(g_b_one).reshape(folds, parts, unit), (1, 0, 2))
    bias_partial = jnp.concatenate(
        [
            jnp.where(mine[:, None], g_b_q[None], 0.0).reshape(inner),
            jnp.where(mine[:, None], g_b_v[None], 0.0).reshape(inner),
            g_b_proj,
            jnp.where(mine[None, :, None, None], units_one[:, None], 0.0).reshape(FF),
            g_b_fc2,
            d_mod,
        ]
    )
    chunk = bias_partial.shape[0] // devices
    bias_terms = lax.all_to_all(
        bias_partial.reshape(devices, chunk), axes, split_axis=0, concat_axis=0, tiled=True
    )
    bias_chunk = jnp.sum(bias_terms, axis=0)

    count_ada = width // replicas
    own_ada = lax.dynamic_slice_in_dim(g_ada, rank * count_ada, count_ada, 1)
    far_mlp = swap(grads_mlp) if replicas == 2 else jnp.zeros_like(grads_mlp)
    both_mlp = jnp.where(turn == 0, jnp.stack([grads_mlp, far_mlp]), jnp.stack([far_mlp, grads_mlp]))
    full_one = both_mlp[:, :, : folds * width].reshape(2, rows, folds, parts, unit)
    full_one = jnp.transpose(full_one, (1, 3, 0, 2, 4)).reshape(rows, FF)
    full_two = both_mlp[:, :, folds * width :].reshape(2, rows, folds, width)
    full_two = jnp.transpose(full_two, (0, 2, 1, 3)).reshape(2 * folds * rows, width)

    weights = (w_qkv, w_proj, w_fc1, w_fc2, w_ada.T)
    if replicas == 2:
        early = sum((jnp.sum(jnp.square(g.astype(jnp.float32))) for g in (grads_mlp, own_ada)))
        early = early + jnp.sum(bias_chunk * bias_chunk)
        grads_attn, full_one, full_two, g_ada, early = lax.optimization_barrier(
            (grads_attn, full_one, full_two, g_ada, early)
        )
        counted = [grads_attn.astype(jnp.float32)]
    else:
        blank = jnp.zeros_like(grads_attn)
        both = ordered(grads_attn[None], blank[None], 0)
        full_proj = jnp.transpose(both[:, :, :half], (1, 0, 2)).reshape(rows, inner)
        full_qkv = both[:, :, proj_wide:].reshape(2, rows, 3, half)
        full_qkv = jnp.transpose(full_qkv, (1, 2, 0, 3)).reshape(rows, 3 * inner)
        pieces = [
            lax.psum_scatter(full.astype(jnp.float32), "rep", scatter_dimension=1, tiled=True)
            for full in (full_qkv, full_proj, full_one, full_two)
        ] + [own_ada]
        counted = pieces
        early = jnp.sum(bias_chunk * bias_chunk)
    squares = sum((jnp.sum(p * p) for p in counted)) + early
    totals = spread(jnp.concatenate([bias_chunk, squares[None]])[None])
    g_bias = totals[:, :chunk].reshape(devices * chunk)
    gnorm = jnp.sqrt(jnp.sum(totals[:, chunk]))
    clip = 1.0 / jnp.maximum(gnorm, 1.0)

    new_w = []
    new_m = []
    new_v = []
    if replicas == 2:
        far_attn = swap(grads_attn)
        scalars = (clip.reshape(1), turn.reshape(1).astype(jnp.int32))
        pair_attn = (grads_attn, far_attn)
        sources = (pair_attn, pair_attn, (full_one,), (full_two,), (g_ada,))
        plans = (
            (
                half,
                [
                    (half * b, b % 2, proj_wide + half * (b // 2), b // 3, half * (b % 3))
                    for b in range(6)
                ],
            ),
            (half, [(half * b, b, 0, b, 0) for b in range(2)]),
            (FF // 2, [(FF // 2 * b, -1, FF // 2 * b, b, 0) for b in range(2)]),
            (half, [(half * b, -1, half * b, b, 0) for b in range(2)]),
            (count_ada, [(count_ada * b, -1, count_ada * b, b, 0) for b in range(2)]),
        )
        for k, (weight, grads, plan) in enumerate(zip(weights, sources, plans)):
            updated, first_new, second_new = update_both(
                weight, grads, firsts[k], seconds[k], fars[k], fars[5 + k], scalars, plan
            )
            new_w.append(updated)
            new_m.append(first_new)
            new_v.append(second_new)
    else:
        for weight, grad, first, second in zip(weights, pieces, firsts, seconds):
            count = weight.shape[1] // replicas
            own = lax.dynamic_slice_in_dim(weight, rank * count, count, 1)
            change, first_new, second_new = adam_change(own, grad, first, second, clip)
            changes = lax.all_gather(change.astype(jnp.bfloat16), "rep", axis=1, tiled=True)
            new_w.append(weight + changes.astype(jnp.float32))
            new_m.append(first_new)
            new_v.append(second_new)
    new_w[4], new_m[4], new_v[4] = new_w[4].T, new_m[4].T, new_v[4].T
    bias_update, new_m_bias, new_v_bias = adam_change(biases, g_bias, m_bias, v_bias, clip)
    return (
        block_out,
        latents_grad,
        cond_grad,
        *new_w,
        bias_update,
        *new_m,
        new_m_bias,
        *new_v,
        new_v_bias,
    )


def solution(mesh):
    in_specs = (
        P(("rep", "shard"), None, None),
        P(("rep", "shard"), None),
        P(("rep", "shard")),
        P(("rep", "shard"), None, None),
        P("shard", None),
        P("shard", None),
        P("shard", None),
        P("shard", None),
        P(None, "shard"),
        P(),
        P("shard", "rep"),
        P("shard", "rep"),
        P("shard", "rep"),
        P("shard", "rep"),
        P("rep", "shard"),
        P(),
        P("shard", "rep"),
        P("shard", "rep"),
        P("shard", "rep"),
        P("shard", "rep"),
        P("rep", "shard"),
        P(),
    )
    out_specs = (
        P(("rep", "shard"), None, None),
        P(("rep", "shard"), None, None),
        P(("rep", "shard"), None),
        P("shard", None),
        P("shard", None),
        P("shard", None),
        P("shard", None),
        P(None, "shard"),
        P(),
        P("shard", "rep"),
        P("shard", "rep"),
        P("shard", "rep"),
        P("shard", "rep"),
        P("rep", "shard"),
        P(),
        P("shard", "rep"),
        P("shard", "rep"),
        P("shard", "rep"),
        P("shard", "rep"),
        P("rep", "shard"),
        P(),
    )
    return jax.shard_map(shards, mesh=mesh, in_specs=in_specs, out_specs=out_specs, check_vma=False)
```

```python
import math

import jax
import jax.numpy as jnp
from jax import lax
from jax.experimental import pallas as pl
from jax.experimental.pallas import tpu as pltpu
from jax.sharding import PartitionSpec as P

HD = 72
H = 16
FF = 4608


ln_eps = 1e-06
beta_one = 0.9
beta_two = 0.999
adam_eps = 1e-08
learn_rate = 0.03
decay_rate = 0.01
step_count = 2
gelu_coef = 0.044715


def product(form, left, right):
    return jnp.einsum(form, left, right, preferred_element_type=jnp.float32)


def normalize(rows):
    center = rows - jnp.mean(rows, axis=-1, keepdims=True)
    rstd = lax.rsqrt(jnp.mean(center * center, axis=-1, keepdims=True) + ln_eps)
    return (center * rstd, rstd)


def norm_back(grad, normed, rstd):
    return rstd * (
        grad
        - jnp.mean(grad, axis=-1, keepdims=True)
        - normed * jnp.mean(grad * normed, axis=-1, keepdims=True)
    )


def gelu_parts(pre):
    root = math.sqrt(2.0 / math.pi)
    inner = root * (pre + gelu_coef * pre * pre * pre)
    tangent = jnp.tanh(inner)
    value = 0.5 * pre * (1.0 + tangent)
    slope = 0.5 * (1.0 + tangent) + 0.5 * pre * (1.0 - tangent * tangent) * root * (
        1.0 + 3.0 * gelu_coef * pre * pre
    )
    return (value, slope)


def time_embed(steps, width):
    half = width // 2
    freqs = jnp.exp(-math.log(10000.0) * jnp.arange(half, dtype=jnp.float32) / half)
    angles = steps.astype(jnp.float32)[:, None] * freqs[None, :]
    return jnp.concatenate([jnp.cos(angles), jnp.sin(angles)], axis=1)


def adam_change(weight, grad, first, second, clip):
    scaled = grad * clip
    first_new = beta_one * first + (1.0 - beta_one) * scaled
    second_new = beta_two * second + (1.0 - beta_two) * scaled * scaled
    first_hat = first_new / (1.0 - beta_one**step_count)
    second_hat = second_new / (1.0 - beta_two**step_count)
    change = -learn_rate * (first_hat / (jnp.sqrt(second_hat) + adam_eps) + decay_rate * weight)
    return (change, first_new, second_new)


def outer(left, right):
    return lax.dot_general(
        left, right, (((0,), (0,)), ((), ())), preferred_element_type=jnp.float32
    ).astype(jnp.bfloat16)


def pack_products(pairs, picks, starts, total, block):
    lefts, rights = pairs
    tall, width = lefts[0].shape
    wide = total // len(picks)

    def body(*refs):
        step = pl.program_id(0)
        out = refs[-1]
        for j, writes in enumerate(picks):

            @pl.when(step == j)
            def _():
                for left, right, column in writes:
                    value = outer(refs[left][...], refs[len(lefts) + right][...])
                    out[:, column : column + value.shape[1]] = value

    return pl.pallas_call(
        body,
        grid=(len(picks), width // block),
        in_specs=[pl.BlockSpec((tall, block), lambda j, i: (0, i)) for _ in lefts]
        + [pl.BlockSpec(r.shape, lambda j, i: (0, 0)) for r in rights],
        out_specs=pl.BlockSpec((block, wide), lambda j, i: (i, j)),
        out_shape=jax.ShapeDtypeStruct((width, total), jnp.bfloat16),
        name=starts,
    )(*lefts, *rights)


def update_both(weight, grads, first, second, first_far, second_far, scalars, plan):
    size, blocks = plan
    clip, turn = scalars

    def cut(ref, start):
        return ref[:, start : start + size]

    def put(ref, start, value):
        ref[:, start : start + size] = value

    def body(clip_ref, turn_ref, w_ref, *refs):
        g_refs = refs[: len(grads)]
        m_ref, v_ref, mf_ref, vf_ref, w_out, m_out, v_out = refs[len(grads) :]
        scale = clip_ref[0]
        for place in (0, 1):

            @pl.when(turn_ref[0] == place)
            def _():
                for w_at, g_member, g_at, m_member, m_at in blocks:
                    source = g_refs[0] if g_member in (-1, place) else g_refs[1]
                    grad = cut(source, g_at).astype(jnp.float32) * scale
                    own = m_member == place
                    first_old = cut(m_ref if own else mf_ref, m_at)
                    second_old = cut(v_ref if own else vf_ref, m_at)
                    if own:
                        put(m_out, m_at, beta_one * first_old + (1.0 - beta_one) * grad)
                        put(v_out, m_at, beta_two * second_old + (1.0 - beta_two) * grad * grad)
                        first_old = first_old.astype(jnp.bfloat16)
                        second_old = second_old.astype(jnp.bfloat16)
                    first_new = beta_one * first_old.astype(jnp.float32) + (1.0 - beta_one) * grad
                    second_new = (
                        beta_two * second_old.astype(jnp.float32) + (1.0 - beta_two) * grad * grad
                    )
                    first_hat = first_new * (1.0 / (1.0 - beta_one**step_count))
                    second_hat = second_new * (1.0 / (1.0 - beta_two**step_count))
                    old = cut(w_ref, w_at)
                    change = -learn_rate * (
                        first_hat / (jnp.sqrt(second_hat) + adam_eps) + decay_rate * old
                    )
                    put(w_out, w_at, old + change)

    vmem = pl.BlockSpec(memory_space=pltpu.VMEM)
    smem = pl.BlockSpec(memory_space=pltpu.SMEM)
    return pl.pallas_call(
        body,
        in_specs=[smem, smem] + [vmem] * (5 + len(grads)),
        out_specs=[vmem] * 3,
        out_shape=[jax.ShapeDtypeStruct(a.shape, a.dtype) for a in (weight, first, second)],
        name="update",
    )(clip, turn, weight, *grads, first, second, first_far, second_far)


def shards(
    latents,
    cond,
    timesteps,
    cotangent,
    w_qkv,
    w_proj,
    w_fc1,
    w_fc2,
    w_ada,
    biases,
    m_qkv,
    m_proj,
    m_fc1,
    m_fc2,
    m_ada,
    m_bias,
    v_qkv,
    v_proj,
    v_fc1,
    v_fc2,
    v_ada,
    v_bias,
):
    axes = ("rep", "shard")
    replicas = lax.axis_size("rep")
    parts = lax.axis_size("shard")
    devices = replicas * parts
    rank = lax.axis_index("rep")
    turn = rank % 2
    couples = [(i, i ^ 1) for i in range(replicas)]
    length, width = latents.shape[1:]
    inner = H * HD
    half = inner // 2
    heads = H // 2
    rows = w_qkv.shape[0]
    folds = FF // (2 * width)
    unit = FF // (2 * parts * folds)

    def swap(value):
        return lax.ppermute(value, "rep", couples)

    def ordered(own, other, axis):
        first = jnp.concatenate([own, other], axis=axis)
        second = jnp.concatenate([other, own], axis=axis)
        return jnp.where(turn == 0, first, second)

    def own_half(value, axis):
        count = value.shape[axis] // 2
        return lax.dynamic_slice_in_dim(value, turn * count, count, axis)

    def spread(value):
        copies = jnp.broadcast_to(value, (devices,) + value.shape[1:])
        return lax.all_to_all(copies, axes, split_axis=0, concat_axis=0, tiled=True)

    b_q = own_half(biases[0:inner], 0)
    b_v = own_half(biases[inner : 2 * inner], 0)
    b_proj = biases[2 * inner : 2 * inner + width]
    b_fc1 = biases[2 * inner + width : 2 * inner + width + FF]
    b_fc2 = biases[2 * inner + width + FF : 2 * inner + 2 * width + FF]
    b_ada = biases[biases.shape[0] - 6 * width :]
    units = lax.dynamic_index_in_dim(
        b_fc1.reshape(parts, 2, folds, unit), turn, 1, keepdims=False
    )
    b_one = jnp.transpose(units, (1, 0, 2)).reshape(folds, width)

    wq_half = own_half(w_qkv.astype(jnp.bfloat16).reshape(rows, 3, inner), 2)
    w1_half = lax.dynamic_index_in_dim(
        w_fc1.astype(jnp.bfloat16).reshape(rows, parts, 2, folds, unit), turn, 2, keepdims=False
    )
    w1_half = jnp.transpose(w1_half, (0, 2, 1, 3)).reshape(rows, folds * width)
    pack_first = jnp.concatenate(
        [w_proj.astype(jnp.bfloat16), w1_half, wq_half.reshape(rows, 3 * half)], axis=1
    )
    full_first = lax.all_gather(pack_first, "shard", axis=0, tiled=True)
    w2_half = own_half(w_fc2.astype(jnp.bfloat16), 0).reshape(folds, rows, width)
    pack_second = jnp.concatenate([w2_half[f] for f in range(folds)], axis=1)
    full_second = lax.all_gather(pack_second, "shard", axis=0, tiled=True)
    firsts = (m_qkv, m_proj, m_fc1, m_fc2, m_ada.T)
    seconds = (v_qkv, v_proj, v_fc1, v_fc2, v_ada.T)
    fars = []
    if replicas == 2:
        fars = [swap(value.astype(jnp.bfloat16)) for value in firsts + seconds]
    full_first, fars = lax.optimization_barrier((full_first, fars))
    wp_b = full_first[:, :width]
    w1_b = [full_first[:, (1 + f) * width : (2 + f) * width] for f in range(folds)]
    wq_b = full_first[:, (1 + folds) * width :]

    cvec = cond + time_embed(timesteps, width)
    silu_c = jax.nn.silu(cvec).astype(jnp.bfloat16)
    ada_local = w_ada.astype(jnp.bfloat16)
    silu_all = spread(silu_c)
    silu_group = lax.dynamic_slice_in_dim(silu_all, rank * parts, parts, 0)
    mod_cols = jnp.dot(silu_group, ada_local, preferred_element_type=jnp.float32)
    mod = lax.all_to_all(mod_cols, "shard", split_axis=0, concat_axis=1, tiled=True) + b_ada
    shift1, scale1, gate1, shift2, scale2, gate2 = [
        mod[:, i * width : (i + 1) * width] for i in range(6)
    ]

    tokens = latents[0].astype(jnp.float32)
    n_one, r_one = normalize(tokens)
    a_one = (n_one * (1.0 + scale1) + shift1).astype(jnp.bfloat16)
    grad_out = cotangent[0].astype(jnp.float32)
    d_mlp = grad_out * gate2
    d_mlp_b = d_mlp.astype(jnp.bfloat16)
    a_one2 = jnp.concatenate([a_one, swap(a_one)], axis=0)
    d_mlp2 = jnp.concatenate([d_mlp_b, swap(d_mlp_b)], axis=0)

    qkv = product("ld,de->le", a_one2, wq_b)
    shape = (2, length, heads, HD)
    queries = (qkv[:, :half] + b_q).astype(jnp.bfloat16).reshape(shape)
    key_rows = qkv[:, half : 2 * half].astype(jnp.bfloat16).reshape(shape)
    value_rows = (qkv[:, 2 * half :] + b_v).astype(jnp.bfloat16).reshape(shape)
    factor = HD ** (-0.5)
    scores = product("bqhd,bkhd->bhqk", queries, key_rows) * factor
    top = jnp.max(scores, axis=-1, keepdims=True)
    expo = jnp.exp(scores - top)
    probs = expo / jnp.sum(expo, axis=-1, keepdims=True)
    probs_b = probs.astype(jnp.bfloat16)
    heads_out = product("bhqk,bkhd->bqhd", probs_b, value_rows).astype(jnp.bfloat16)
    heads_flat = heads_out.reshape(2, length, half)
    heads_other = swap(heads_flat)[::-1]
    heads_own = ordered(heads_flat[0], heads_other[0], 1)
    attn = product("le,ed->ld", heads_own, wp_b) + b_proj
    x_one = tokens + gate1 * attn
    n_two, r_two = normalize(x_one)
    a_two = (n_two * (1.0 + scale2) + shift2).astype(jnp.bfloat16)
    a_two2 = jnp.concatenate([a_two, swap(a_two)], axis=0)

    acts = []
    slopes = []
    for f in range(folds):
        pre = product("ld,df->lf", a_two2, w1_b[f]) + b_one[f]
        act_val, act_slope = gelu_parts(pre)
        acts.append(act_val.astype(jnp.bfloat16))
        slopes.append(act_slope)
    pack_two = pack_products(
        (acts, [d_mlp2]), [[(f, 0, 0)] for f in range(folds)], "pack_two", folds * width, width
    )
    grads_two = lax.psum_scatter(pack_two, "shard", scatter_dimension=0, tiled=True)
    full_second, slopes, pack_two = lax.optimization_barrier((full_second, slopes, pack_two))
    w2_b = [full_second[:, f * width : (f + 1) * width] for f in range(folds)]
    d_a2_sum = 0.0
    d_pres = []
    g_b_one = []
    for f in range(folds):
        d_pre = product("ld,fd->lf", d_mlp2, w2_b[f]) * slopes[f]
        d_pre_b = d_pre.astype(jnp.bfloat16)
        d_a2_sum = d_a2_sum + product("lf,df->ld", d_pre_b, w1_b[f])
        d_pres.append(d_pre_b)
        g_b_one.append(jnp.sum(d_pre, axis=0))
    d_a2_far = swap(d_a2_sum[length:].astype(jnp.bfloat16))
    d_a2 = d_a2_sum[:length] + d_a2_far.astype(jnp.float32)
    d_shift2 = jnp.sum(d_a2, axis=0)
    d_scale2 = jnp.sum(d_a2 * n_two, axis=0)
    dx_one = grad_out + norm_back(d_a2 * (1.0 + scale2), n_two, r_two)
    d_gate1 = jnp.sum(dx_one * attn, axis=0)
    d_attn = dx_one * gate1
    d_attn_b = d_attn.astype(jnp.bfloat16)
    g_b_proj = jnp.sum(d_attn, axis=0)
    d_attn2 = jnp.concatenate([d_attn_b, swap(d_attn_b)], axis=0)
    d_heads = (
        product("ld,ed->le", d_attn2, own_half(wp_b, 0)).astype(jnp.bfloat16).reshape(shape)
    )
    heads_all = jnp.concatenate(
        [heads_own, ordered(heads_flat[1], heads_other[1], 1)], axis=0
    )
    delta = jnp.sum(d_heads.astype(jnp.float32) * heads_out.astype(jnp.float32), axis=-1)
    delta = jnp.transpose(delta, (0, 2, 1))[..., None]
    d_probs = product("bqhd,bkhd->bhqk", d_heads, value_rows)
    d_scores = (probs * (d_probs - delta) * factor).astype(jnp.bfloat16)
    d_q = product("bhqk,bkhd->bqhd", d_scores, key_rows)
    d_k = product("bhqk,bqhd->bkhd", d_scores, queries)
    d_v = product("bhqk,bqhd->bkhd", probs_b, d_heads)
    g_b_q = jnp.sum(d_q, axis=(0, 1)).reshape(half)
    g_b_v = jnp.sum(d_v, axis=(0, 1)).reshape(half)
    d_qkv = jnp.concatenate(
        [piece.astype(jnp.bfloat16).reshape(2 * length, half) for piece in (d_q, d_k, d_v)],
        axis=1,
    )
    proj_wide = -(-half // 128) * 128
    d_attn_half = jnp.pad(own_half(d_attn2, 1), ((0, 0), (0, proj_wide - half)))
    one_wide = folds * width
    picks = [(0, f, f * width) for f in range(folds)]
    picks += [(1, folds, one_wide), (2, folds + 1, one_wide + proj_wide)]
    pack_rest = pack_products(
        ([a_two2, heads_all, a_one2], d_pres + [d_attn_half, d_qkv]),
        [picks],
        "pack_rest",
        one_wide + proj_wide + 3 * half,
        3 * 128,
    )
    grads_two, pack_rest, acts, d_qkv = lax.optimization_barrier(
        (grads_two, pack_rest, acts, d_qkv)
    )
    grads_rest = lax.psum_scatter(pack_rest, "shard", scatter_dimension=0, tiled=True)
    mlp_sum = 0.0
    for f in range(folds):
        mlp_sum = mlp_sum + product("lf,fd->ld", acts[f], w2_b[f])
    mlp = (
        mlp_sum[:length]
        + swap(mlp_sum[length:].astype(jnp.bfloat16)).astype(jnp.float32)
        + b_fc2
    )
    block_out = (x_one + gate2 * mlp)[None]
    d_gate2 = jnp.sum(grad_out * mlp, axis=0)
    g_b_fc2 = jnp.sum(d_mlp, axis=0)

    d_a1_sum = product("le,de->ld", d_qkv, wq_b)
    d_a1 = d_a1_sum[:length] + swap(d_a1_sum[length:].astype(jnp.bfloat16)).astype(jnp.float32)
    d_shift1 = jnp.sum(d_a1, axis=0)
    d_scale1 = jnp.sum(d_a1 * n_one, axis=0)
    latents_grad = (dx_one + norm_back(d_a1 * (1.0 + scale1), n_one, r_one))[None]

    d_mod = jnp.concatenate([d_shift1, d_scale1, d_gate1, d_shift2, d_scale2, d_gate2])
    d_mod_b = d_mod.astype(jnp.bfloat16).reshape(1, parts, d_mod.shape[0] // parts)
    d_mod_b = jnp.broadcast_to(d_mod_b, (replicas,) + d_mod_b.shape[1:])
    d_mod_cols = lax.all_to_all(
        d_mod_b.reshape(devices, d_mod_b.shape[2]), axes, split_axis=0, concat_axis=0, tiled=True
    )
    g_ada = jnp.dot(d_mod_cols.T, silu_all, preferred_element_type=jnp.float32)
    group_cols = lax.dynamic_slice_in_dim(d_mod_cols, rank * parts, parts, 0)
    silu_terms = jnp.dot(group_cols, ada_local.T, preferred_element_type=jnp.float32)
    silu_terms = lax.all_to_all(silu_terms, "shard", split_axis=0, concat_axis=0, tiled=True)
    silu_grad = jnp.sum(silu_terms, axis=0, keepdims=True)
    sig = jax.nn.sigmoid(cvec)
    cond_grad = silu_grad * sig * (1.0 + cvec * (1.0 - sig))

    mine = jnp.arange(2) == turn
    units_one = jnp.transpose(jnp.stack(g_b_one).reshape(folds, parts, unit), (1, 0, 2))
    bias_partial = jnp.concatenate(
        [
            jnp.where(mine[:, None], g_b_q[None], 0.0).reshape(inner),
            jnp.where(mine[:, None], g_b_v[None], 0.0).reshape(inner),
            g_b_proj,
            jnp.where(mine[None, :, None, None], units_one[:, None], 0.0).reshape(FF),
            g_b_fc2,
            d_mod,
        ]
    )
    chunk = bias_partial.shape[0] // devices
    bias_terms = lax.all_to_all(
        bias_partial.reshape(devices, chunk), axes, split_axis=0, concat_axis=0, tiled=True
    )
    bias_chunk = jnp.sum(bias_terms, axis=0)

    count_ada = width // replicas
    own_ada = lax.dynamic_slice_in_dim(g_ada, rank * count_ada, count_ada, 1)
    def pair_of(own, far):
        return jnp.where(turn == 0, jnp.stack([own, far]), jnp.stack([far, own]))

    def full_of_one(own, far):
        full = pair_of(own, far).reshape(2, rows, folds, parts, unit)
        return jnp.transpose(full, (1, 3, 0, 2, 4)).reshape(rows, FF)

    far_two = swap(grads_two) if replicas == 2 else jnp.zeros_like(grads_two)
    full_two = pair_of(grads_two, far_two).reshape(2, rows, folds, width)
    full_two = jnp.transpose(full_two, (0, 2, 1, 3)).reshape(2 * folds * rows, width)

    weights = (w_qkv, w_proj, w_fc1, w_fc2, w_ada.T)
    if replicas == 2:
        early = sum((jnp.sum(jnp.square(g.astype(jnp.float32))) for g in (grads_two, own_ada)))
        early = early + jnp.sum(bias_chunk * bias_chunk)
        grads_rest, full_two, g_ada, early = lax.optimization_barrier(
            (grads_rest, full_two, g_ada, early)
        )
        counted = [grads_rest.astype(jnp.float32)]
    else:
        grads_attn = grads_rest[:, one_wide:]
        full_one = full_of_one(grads_rest[:, :one_wide], jnp.zeros_like(grads_two))
        blank = jnp.zeros_like(grads_attn)
        both = ordered(grads_attn[None], blank[None], 0)
        full_proj = jnp.transpose(both[:, :, :half], (1, 0, 2)).reshape(rows, inner)
        full_qkv = both[:, :, proj_wide:].reshape(2, rows, 3, half)
        full_qkv = jnp.transpose(full_qkv, (1, 2, 0, 3)).reshape(rows, 3 * inner)
        pieces = [
            lax.psum_scatter(full.astype(jnp.float32), "rep", scatter_dimension=1, tiled=True)
            for full in (full_qkv, full_proj, full_one, full_two)
        ] + [own_ada]
        counted = pieces
        early = jnp.sum(bias_chunk * bias_chunk)
    squares = sum((jnp.sum(p * p) for p in counted)) + early
    totals = spread(jnp.concatenate([bias_chunk, squares[None]])[None])
    g_bias = totals[:, :chunk].reshape(devices * chunk)
    gnorm = jnp.sqrt(jnp.sum(totals[:, chunk]))
    clip = 1.0 / jnp.maximum(gnorm, 1.0)

    new_w = []
    new_m = []
    new_v = []
    if replicas == 2:
        far_rest = swap(grads_rest)
        full_one = full_of_one(grads_rest[:, :one_wide], far_rest[:, :one_wide])
        scalars = (clip.reshape(1), turn.reshape(1).astype(jnp.int32))
        qkv_at = one_wide + proj_wide
        pair_attn = (grads_rest, far_rest)
        sources = (pair_attn, pair_attn, (full_one,), (full_two,), (g_ada,))
        plans = (
            (
                half,
                [
                    (half * b, b % 2, qkv_at + half * (b // 2), b // 3, half * (b % 3))
                    for b in range(6)
                ],
            ),
            (half, [(half * b, b, one_wide, b, 0) for b in range(2)]),
            (FF // 2, [(FF // 2 * b, -1, FF // 2 * b, b, 0) for b in range(2)]),
            (half, [(half * b, -1, half * b, b, 0) for b in range(2)]),
            (count_ada, [(count_ada * b, -1, count_ada * b, b, 0) for b in range(2)]),
        )
        for k, (weight, grads, plan) in enumerate(zip(weights, sources, plans)):
            updated, first_new, second_new = update_both(
                weight, grads, firsts[k], seconds[k], fars[k], fars[5 + k], scalars, plan
            )
            new_w.append(updated)
            new_m.append(first_new)
            new_v.append(second_new)
    else:
        for weight, grad, first, second in zip(weights, pieces, firsts, seconds):
            count = weight.shape[1] // replicas
            own = lax.dynamic_slice_in_dim(weight, rank * count, count, 1)
            change, first_new, second_new = adam_change(own, grad, first, second, clip)
            changes = lax.all_gather(change.astype(jnp.bfloat16), "rep", axis=1, tiled=True)
            new_w.append(weight + changes.astype(jnp.float32))
            new_m.append(first_new)
            new_v.append(second_new)
    new_w[4], new_m[4], new_v[4] = new_w[4].T, new_m[4].T, new_v[4].T
    bias_update, new_m_bias, new_v_bias = adam_change(biases, g_bias, m_bias, v_bias, clip)
    return (
        block_out,
        latents_grad,
        cond_grad,
        *new_w,
        bias_update,
        *new_m,
        new_m_bias,
        *new_v,
        new_v_bias,
    )


def solution(mesh):
    in_specs = (
        P(("rep", "shard"), None, None),
        P(("rep", "shard"), None),
        P(("rep", "shard")),
        P(("rep", "shard"), None, None),
        P("shard", None),
        P("shard", None),
        P("shard", None),
        P("shard", None),
        P(None, "shard"),
        P(),
        P("shard", "rep"),
        P("shard", "rep"),
        P("shard", "rep"),
        P("shard", "rep"),
        P("rep", "shard"),
        P(),
        P("shard", "rep"),
        P("shard", "rep"),
        P("shard", "rep"),
        P("shard", "rep"),
        P("rep", "shard"),
        P(),
    )
    out_specs = (
        P(("rep", "shard"), None, None),
        P(("rep", "shard"), None, None),
        P(("rep", "shard"), None),
        P("shard", None),
        P("shard", None),
        P("shard", None),
        P("shard", None),
        P(None, "shard"),
        P(),
        P("shard", "rep"),
        P("shard", "rep"),
        P("shard", "rep"),
        P("shard", "rep"),
        P("rep", "shard"),
        P(),
        P("shard", "rep"),
        P("shard", "rep"),
        P("shard", "rep"),
        P("shard", "rep"),
        P("rep", "shard"),
        P(),
    )
    return jax.shard_map(shards, mesh=mesh, in_specs=in_specs, out_specs=out_specs, check_vma=False)
```
